128 devices in a mesh: src: 8 (over x_hi, y), ch: 16 (over z, x_lo, core).
Axes of the slice: x: 4 (x_hi: 2, x_lo: 2; x = x_hi * 2 + x_lo), y: 4, z: 4, core: 2. Of those that a mesh axis runs over, the one named last changes fastest.
Arguments:
- dry_signal: bfloat16 [128, 40960], P(('src', 'ch')), may hold values from -6 to 6
- room_spectra: bfloat16 [128, 8, 64, 2, 1024], P('src', None, 'ch'), may hold values from -0.125 to 0.125
- render_slot: int32 [128], P('src'), may hold values from 0 to 127, as said below
- decoder: bfloat16 [64, 1024], replicated, may hold values from -0.75 to 0.75
Outputs:
- speakers: bfloat16 [32768, 1024], P(('src', 'ch'))
The draws below stay inside these ranges and needn't reach their ends.
Inputs may be any that keep to these rules, and one draw needn't show every extreme that they name: render_slot is a permutation that keeps each group: sources g * 16 to (g + 1) * 16 - 1 are mapped onto the rows of that same range, each row once.
All inputs are finite; a program needn't handle non-finite values.
Results may differ from the reference program's by a relative error of at most 0.018.
Values may be sent and summed in bfloat16 or wider, within the bound.
A program may use at most 128 MiB of HBM per device.

```python
import math
import jax
import jax.numpy as jnp
from jax import lax

CH = 64
BLOCK = 1024
PARTITIONS = 8
SPK = 1024
GROUP = 16
NBLK = 32
SOURCES = 128


def draw_render_slot(key, part):
    groups = SOURCES // GROUP
    subkeys = jax.random.split(key, groups)
    orders = jax.vmap(lambda subkey: jax.random.permutation(subkey, GROUP))(subkeys)
    offsets = jnp.arange(groups, dtype=jnp.int32)[:, None] * GROUP
    return (orders.astype(jnp.int32) + offsets).reshape(SOURCES)


def steps_of(key, shape, shards, least, top_value):
    def one(dim, shards_of):
        steps = jax.random.uniform(jax.random.fold_in(jax.random.fold_in(key, 6), dim), (shards_of,), jnp.float32, least / len(shards), top_value / len(shards))
        return jnp.repeat(jnp.exp(steps), shape[dim] // shards_of).reshape((-1,) + (1,) * (len(shape) - dim - 1))

    loudness = one(*shards[0])
    for cut in shards[1:]:
        loudness = loudness * one(*cut)
    return loudness


def gaussian(stream_key, extent, scale, most, cuts=(), kind=jnp.bfloat16):
    entries = jax.random.normal(stream_key, extent, jnp.float32) * scale
    if len(cuts) > 0:
        entries = steps_of(stream_key, extent, cuts, -0.22, 0.18) * entries
    return jnp.clip(entries, min=-most, max=most).astype(kind)


def setup_inputs(seed: int = 0) -> dict:
    key_of = jax.random.split(jax.random.key(seed), 5)
    return {
        "dry_signal": gaussian(key_of[0], (SOURCES, (NBLK + PARTITIONS) * BLOCK), 1.0, 6.0, ((0, 128),)),
        "room_spectra": gaussian(key_of[1], (SOURCES, PARTITIONS, CH, 2, BLOCK), (2 * SOURCES * PARTITIONS) ** -0.5, 0.125, ((0, 8), (2, 16))),
        "render_slot": draw_render_slot(jax.random.fold_in(key_of[4], 71), 0),
        "decoder": gaussian(key_of[3], (CH, SPK), CH ** -0.5, 0.75),
    }


def make_tables(block_len):
    size = 2 * block_len
    rows = jnp.arange(size, dtype=jnp.int32)[:, None]
    bins = jnp.arange(block_len, dtype=jnp.int32)[None, :]
    phase = ((rows * bins) % size).astype(jnp.float32) * (2.0 * math.pi / size)
    signs = (1 - 2 * (rows % 2)).astype(jnp.float32)
    fwd_imag = jnp.where(bins == 0, signs, -jnp.sin(phase))
    fwd_table = jnp.stack([jnp.cos(phase), fwd_imag], axis=1).astype(jnp.bfloat16)
    freq = jnp.arange(block_len, dtype=jnp.int32)[:, None]
    times = jnp.arange(block_len, dtype=jnp.int32)[None, :] + block_len
    angle = ((freq * times) % size).astype(jnp.float32) * (2.0 * math.pi / size)
    weight = jnp.where(freq == 0, 1.0, 2.0).astype(jnp.float32)
    inv_real = weight * jnp.cos(angle) / size
    tsign = (1 - 2 * (times % 2)).astype(jnp.float32) / size
    inv_imag = jnp.where(freq == 0, tsign, -2.0 * jnp.sin(angle) / size)
    inv_table = jnp.stack([inv_real, inv_imag], axis=0)
    return fwd_table, inv_table


def reference(dry_signal, room_spectra, render_slot, decoder):
    blocks = dry_signal.reshape(SOURCES, NBLK + PARTITIONS, BLOCK)
    frames = jnp.concatenate([blocks[:, :-1], blocks[:, 1:]], axis=-1)
    fwd_table, inv_table = make_tables(BLOCK)
    spectra = jnp.einsum("sfn,njk->sfjk", frames.astype(jnp.float32), fwd_table.astype(jnp.float32),
                         precision=lax.Precision.HIGHEST).astype(jnp.bfloat16)
    ordered = jnp.zeros_like(spectra).at[render_slot].set(spectra)
    bin_index = jnp.arange(BLOCK, dtype=jnp.int32)
    bin_mask = (bin_index > 0).astype(jnp.float32)
    mix_real = jnp.zeros((CH, NBLK, BLOCK), jnp.float32)
    mix_imag = jnp.zeros((CH, NBLK, BLOCK), jnp.float32)
    for p in range(PARTITIONS):
        window = ordered[:, PARTITIONS - 1 - p:PARTITIONS - 1 - p + NBLK].astype(jnp.float32)
        response = room_spectra[:, p].astype(jnp.float32)
        spec_real = window[:, :, 0]
        spec_imag = window[:, :, 1]
        resp_real = response[:, :, 0]
        resp_imag = response[:, :, 1]
        resp_masked = resp_imag * bin_mask
        resp_mixed = jnp.where(bin_index == 0, resp_imag, resp_real)

        def product_sum(left, right):
            return jnp.einsum("sbk,sck->cbk", left, right, precision=lax.Precision.HIGHEST)

        mix_real = mix_real + product_sum(spec_real, resp_real) - product_sum(spec_imag, resp_masked)
        mix_imag = mix_imag + product_sum(spec_real, resp_masked) + product_sum(spec_imag, resp_mixed)
    sh_sum = jnp.einsum("cbk,km->cbm", mix_real, inv_table[0])
    sh_sum = sh_sum + jnp.einsum("cbk,km->cbm", mix_imag, inv_table[1])
    sh_signal = sh_sum.reshape(CH, NBLK * BLOCK).astype(jnp.bfloat16)
    return jnp.dot(sh_signal.T, decoder, preferred_element_type=jnp.float32).astype(jnp.bfloat16)
```

```python
import functools

import numpy as np
import jax, jax.numpy as jnp
from jax import lax
from jax.experimental import pallas as pl
from jax.experimental.pallas import tpu as pltpu
from jax.sharding import PartitionSpec as P

MESH = pl.DeviceIdType.MESH

def trig_tables(block):
    size = 2 * block
    n = 32
    k = np.arange(block)
    lo = 2 * np.pi * ((np.arange(n)[:, None] * k) % size) / size
    hi = 2 * np.pi * ((np.arange(n)[:, None] * n * k) % size) / size
    return np.stack([np.cos(hi), np.sin(hi), np.cos(lo), np.sin(lo)]).astype(np.float32)

def tree(xs):
    while len(xs) > 1:
        xs = [a + b for a, b in zip(xs[::2], xs[1::2])] + ([xs[-1]] if len(xs) % 2 else [])
    return xs[0]

def compute(slot_ref, trig_ref, g_ref, w_hbm, out_ref, w_ref, table, z, zs, spec, swap, acc, accs, mix, w_sem):
    R, PC, CC, B, NB = 16, 8, 4, 1024, 32
    F = NB + PC
    fetch = [pltpu.make_async_copy(w_hbm.at[:, pl.ds(8 * e, 8), :], w_ref.at[:, :, pl.ds(128 * e, 128)], w_sem.at[e]) for e in range(2)]
    for cp in fetch:
        cp.start()
    lane = lax.broadcasted_iota(jnp.int32, (8, 256), 1)
    sigma = (1 - 2 * (lane % 2)).astype(jnp.float32)

    def gen(i, _):
        ca, sa = trig_ref[0, pl.ds(i, 1), :], trig_ref[1, pl.ds(i, 1), :]
        cb, sb = trig_ref[2], trig_ref[3]
        cos = ca * cb - sa * sb
        sin = sa * cb + ca * sb
        k = lax.broadcasted_iota(jnp.int32, (32, B), 1)
        n = lax.broadcasted_iota(jnp.int32, (32, B), 0)
        alt = (1 - 2 * (n % 2)).astype(jnp.float32)
        rows = pl.ds(pl.multiple_of(i * 32, 32), 32)
        table[rows, :B] = cos.astype(jnp.bfloat16)
        table[rows, B:] = jnp.where(k == 0, alt, -sin).astype(jnp.bfloat16)
        return 0
    lax.fori_loop(0, B // 32, gen, 0)
    acc[...] = jnp.zeros_like(acc)
    accs[...] = jnp.zeros_like(accs)

    QS = 4
    def batch(q, _):
        def dft(t, _):
            y = jnp.dot(g_ref[pl.ds(pl.multiple_of(q * (QS * F), 32), QS * F), :],
                        table[:, pl.ds(pl.multiple_of(t * 256, 256), 256)], preferred_element_type=jnp.float32)
            j = t // 4
            for h in range(2):
                kt = (t % 4) * 2 + h
                for i in range(QS * F // 8):
                    v = y[8 * i:8 * i + 8, 128 * h:128 * h + 128]
                    z[pl.ds(i * 128 + kt * 2 + j, 8, stride=16), :] = v
                    zs[pl.ds(i * 128 + kt * 2 + 1 - j, 8, stride=16), :] = v
            return 0
        lax.fori_loop(0, 8, dft, 0)
        def form(s, _):
            for f in range(F - 1):
                o = s * F + f
                def wide(ref, at):
                    at = pl.multiple_of(at, 16)
                    return jnp.concatenate([ref[pl.ds(at, 8), :], ref[pl.ds(at + 8, 8), :]], 1)
                spec[o] = (wide(z, o * 16) + sigma * wide(z, o * 16 + 16)).astype(jnp.bfloat16)
                swap[o] = (wide(zs, o * 16) + sigma * wide(zs, o * 16 + 16)).astype(jnp.bfloat16)
            return 0
        lax.fori_loop(0, QS, form, 0)
        def mixer(i, _):
            pair, c = i // CC, i % CC
            ws = []
            for d in range(2):
                row = slot_ref[q * QS + pair * 2 + d]
                ws.append([w_ref[(row * PC + p) * CC + c] for p in range(PC)])
            def blocks(h, _):
                for bb in range(8):
                    b = h * 8 + bb
                    m1, m2 = [], []
                    for d in range(2):
                        for p in range(PC):
                            o = (pair * 2 + d) * F + b + (PC - 1 - p)
                            m1.append(spec[o] * ws[d][p])
                            m2.append(swap[o] * ws[d][p])
                    o = (b * CC + c)
                    for ref, m in ((acc, m1), (accs, m2)):
                        u = tree(m).astype(jnp.float32)
                        for e in range(2):
                            ref[pl.ds(pl.multiple_of(o * 16 + 8 * e, 8), 8), :] += u[:, 128 * e:128 * e + 128]
                return 0
            lax.fori_loop(0, NB // 8, blocks, 0)
            return 0
        lax.fori_loop(0, QS // 2 * CC, mixer, 0)
        return 0
    for cp in fetch:
        cp.wait()
    lax.fori_loop(0, R // QS, batch, 0)

    lane8 = lax.broadcasted_iota(jnp.int32, (8, 128), 1)
    scale = (1 - 2 * (lane8 % 2)).astype(jnp.float32) * (1.0 / B)
    for kt in range(8):
        sc = jnp.where(lane8 == 0, 0.5 / B, scale) if kt == 0 else scale
        for i in range(0, NB * CC // 8, 2):
            vr, vi = [], []
            for e in (i, i + 1):
                at = lambda ref, j: ref[pl.ds(e * 128 + kt * 2 + j, 8, stride=16), :]
                a, bq, u, v = at(acc, 0), at(acc, 1), at(accs, 0), at(accs, 1)
                re, im = a - bq, u + v
                if kt == 0:
                    re = jnp.where(lane8 == 0, a, re)
                    im = jnp.where(lane8 == 0, bq, im)
                vr.append(re * sc); vi.append(im * sc)
            mix[8 * i:8 * i + 16, kt * 128:kt * 128 + 128] = jnp.concatenate(vr, 0).astype(jnp.bfloat16)
            mix[8 * i:8 * i + 16, B + kt * 128:B + kt * 128 + 128] = jnp.concatenate(vi, 0).astype(jnp.bfloat16)
    for t in range(4):
        y = lax.dot_general(mix[...], table[t * 256:t * 256 + 256, :], (((1,), (1,)), ((), ())), preferred_element_type=jnp.float32)
        for b in range(NB):
            out_ref[b, :, t * 256:t * 256 + 256] = y[CC * b:CC * b + CC, :].astype(jnp.bfloat16)

def convolve(dry, room, slot):
    w = room.reshape(16, 8, 4, 2, 8, 128).transpose(0, 1, 2, 4, 3, 5).reshape(512, 16, 128)
    vm = pl.BlockSpec(memory_space=pltpu.VMEM)
    return pl.pallas_call(
        compute, out_shape=jax.ShapeDtypeStruct((32, 4, 1024), jnp.bfloat16),
        in_specs=[pl.BlockSpec(memory_space=pltpu.SMEM), vm, vm, pl.BlockSpec(memory_space=pl.ANY)], out_specs=vm,
        scratch_shapes=[pltpu.VMEM((512, 8, 256), jnp.bfloat16), pltpu.VMEM((1024, 2048), jnp.bfloat16),
                        pltpu.VMEM((160 * 16, 128), jnp.float32), pltpu.VMEM((160 * 16, 128), jnp.float32),
                        pltpu.VMEM((160, 8, 256), jnp.bfloat16), pltpu.VMEM((160, 8, 256), jnp.bfloat16),
                        pltpu.VMEM((128 * 16, 128), jnp.float32), pltpu.VMEM((128 * 16, 128), jnp.float32),
                        pltpu.VMEM((128, 2048), jnp.bfloat16), pltpu.SemaphoreType.DMA((2,))],
        compiler_params=pltpu.CompilerParams(vmem_limit_bytes=60 * 2**20),
    )(slot, jnp.asarray(trig_tables(1024)), dry, w)


def gather_kernel(n, x_ref, out_ref, own_sem, send_sem, recv_sem):
    me = lax.axis_index("ch")
    rows = x_ref.shape[0]
    barrier = pltpu.get_barrier_semaphore()
    for d in range(1, n):
        pl.semaphore_signal(barrier, inc=1, device_id={"ch": lax.rem(me + d, n)}, device_id_type=MESH)
    pl.semaphore_wait(barrier, n - 1)
    mine = out_ref.at[pl.ds(pl.multiple_of(me * rows, 8), rows), :]
    own = pltpu.make_async_copy(x_ref, mine, own_sem)
    own.start()
    copies = []
    for d in range(1, n):
        cp = pltpu.make_async_remote_copy(src_ref=x_ref, dst_ref=mine, send_sem=send_sem.at[d - 1], recv_sem=recv_sem.at[d - 1],
                                          device_id={"ch": lax.rem(me + d, n)}, device_id_type=MESH)
        cp.start()
        copies.append(cp)
    own.wait()
    for cp in copies:
        cp.wait()


def gather(x, n):
    return pl.pallas_call(
        functools.partial(gather_kernel, n), out_shape=jax.ShapeDtypeStruct((n * x.shape[0], x.shape[1]), x.dtype),
        in_specs=[pl.BlockSpec(memory_space=pltpu.VMEM)], out_specs=pl.BlockSpec(memory_space=pltpu.VMEM),
        scratch_shapes=[pltpu.SemaphoreType.DMA, pltpu.SemaphoreType.DMA((n - 1,)), pltpu.SemaphoreType.DMA((n - 1,))],
        compiler_params=pltpu.CompilerParams(collective_id=0, has_side_effects=True),
    )(x)


def exchange_kernel(ns, nc, x_ref, out_ref, own_sem, send_sem, recv_sem):
    n = ns * nc
    me = lax.axis_index("src") * nc + lax.axis_index("ch")
    parts = n // x_ref.shape[0]
    span = x_ref.shape[2] // parts
    barrier = pltpu.get_barrier_semaphore()

    def hello(d, _):
        t = lax.rem(me + d, n)
        pl.semaphore_signal(barrier, inc=1, device_id=(t // nc, t % nc), device_id_type=MESH)
        return 0

    lax.fori_loop(1, n, hello, 0)
    pl.semaphore_wait(barrier, n - 1)
    chunk = lambda t: x_ref.at[t // parts, :, pl.ds(pl.multiple_of((t % parts) * span, 128), span)]

    def send(d, _):
        t = lax.rem(me + d, n)
        pltpu.make_async_remote_copy(src_ref=chunk(t), dst_ref=out_ref.at[me], send_sem=send_sem, recv_sem=recv_sem,
                                     device_id=(t // nc, t % nc), device_id_type=MESH).start()
        return 0

    lax.fori_loop(1, n, send, 0)
    own = pltpu.make_async_copy(chunk(me), out_ref.at[me], own_sem)
    own.start()
    own.wait()
    rest = out_ref.at[pl.ds(0, n - 1)]
    pltpu.make_async_copy(rest, rest, send_sem).wait()
    pltpu.make_async_copy(rest, rest, recv_sem).wait()


def exchange(x, ns, nc):
    n = ns * nc
    span = x.shape[0] * x.shape[2] // n
    return pl.pallas_call(
        functools.partial(exchange_kernel, ns, nc), out_shape=jax.ShapeDtypeStruct((n, x.shape[1], span), x.dtype),
        in_specs=[pl.BlockSpec(memory_space=pltpu.VMEM)], out_specs=pl.BlockSpec(memory_space=pltpu.VMEM),
        scratch_shapes=[pltpu.SemaphoreType.DMA, pltpu.SemaphoreType.DMA, pltpu.SemaphoreType.DMA],
        compiler_params=pltpu.CompilerParams(collective_id=1, has_side_effects=True),
    )(x)


def solution(mesh):
    ns, nc = mesh.shape["src"], mesh.shape["ch"]

    def per_device(dry, room, slot, decoder):
        dry = gather(dry.reshape(40, 1024), nc)
        sh = convolve(dry, room, slot % room.shape[0])
        parts = exchange(sh, ns, nc)
        total = jnp.sum(parts.reshape(ns, nc * 4, 256).astype(jnp.float32), axis=0).astype(jnp.bfloat16)
        return lax.dot_general(total, decoder, (((0,), (0,)), ((), ())), preferred_element_type=jnp.float32).astype(jnp.bfloat16)

    return jax.shard_map(per_device, mesh=mesh, in_specs=(P(("src", "ch"), None), P("src", None, "ch", None, None), P("src"), P()),
                         out_specs=P(("src", "ch"), None), check_vma=False)
```
